256 devices in a mesh: rep: 16 (over x, z_lo, core), fsdp: 16 (over z_hi, y).
Axes of the slice: x: 4, y: 4, z: 8 (z_hi: 4, z_lo: 2; z = z_hi * 2 + z_lo), core: 2. Of those that a mesh axis runs over, the one named last changes fastest.
Arguments:
- activations: bfloat16 [16, 2, 2816, 2560], P('rep', None, 'fsdp'), may hold values from -6 to 6
- residual: bfloat16 [16, 2, 2816, 5120], P('rep', None, 'fsdp'), may hold values from -6 to 6
- upstream: bfloat16 [16, 2, 2816, 5120], P('rep', None, 'fsdp'), may hold values from -6 to 6
- norm_gain: float32 [5120], replicated, may hold values from 0.5 to 1.5
- params: float32 [16, 128, 40, 5, 128], P('rep', 'fsdp'), may hold values from -6 to 6
- momentum: float32 [16, 128, 40, 5, 128], P('rep', 'fsdp'), may hold values from -6 to 6
- pattern: int32 [40, 5], replicated, may hold values from 0 to 19, as said below
- step_index: int32 [1], replicated, may hold values from 0 to 2999
Outputs:
- params_out: float32 [16, 128, 40, 5, 128], P('rep', 'fsdp')
- momentum_out: float32 [16, 128, 40, 5, 128], P('rep', 'fsdp')
The draws below stay inside these ranges and needn't reach their ends.
Inputs may be any that keep to these rules, and one draw needn't show every extreme that they name: `pattern`: each output block column c lists 5 different input blocks, the first of them c mod 20.
All inputs are finite; a program needn't handle non-finite values.
Results may differ from the reference program's by a relative error of at most 0.012.
Values may be sent and summed in bfloat16 or wider, within the bound.
A program may use at most 128 MiB of HBM per device.

```python
import math
import jax
import jax.numpy as jnp
from jax import lax

D = 5120
HK = 2560
BS = 128
TOK_DEV = 176
STEPS = 2
HB = 20
OB = 40
BPC = 5
TOKENS = 2816
REP = 16
N_FSDP = 16


def draw_pattern(key, part):
    column = jnp.arange(OB, dtype=jnp.int32)
    subkeys = jax.random.split(key, OB)
    offsets = jax.vmap(lambda sub: jax.random.permutation(sub, HB - 1)[:BPC - 1])(subkeys).astype(jnp.int32)
    anchor = column % HB
    chosen = (anchor[:, None] + 1 + offsets) % HB
    return jnp.concatenate([anchor[:, None], chosen], axis=1).astype(jnp.int32)


def shard_levels(key, extent, shards, least, top_value):
    def one(axis_at, shards_of):
        draws = jax.random.uniform(jax.random.fold_in(jax.random.fold_in(key, 6), axis_at), (shards_of,), jnp.float32, least / len(shards), top_value / len(shards))
        return jnp.repeat(jnp.exp(draws), extent[axis_at] // shards_of).reshape((-1,) + (1,) * (len(extent) - axis_at - 1))

    loudness = one(*shards[0])
    for cut in shards[1:]:
        loudness = loudness * one(*cut)
    return loudness


def bell_draw(stream_key, dims, spread, most, pieces=(), kind=jnp.bfloat16):
    level = shard_levels(stream_key, dims, pieces, -0.22, 0.18) if pieces else 1.0
    values = jax.random.normal(stream_key, dims, jnp.float32) * spread * level
    return jnp.minimum(jnp.maximum(values, -most), most).astype(kind)


def setup_inputs(seed: int = 0) -> dict:
    arg_keys = jax.random.split(jax.random.key(seed), 9)
    activations = bell_draw(arg_keys[0], (REP, STEPS, TOKENS, HK), 1.0, 6.0, ((0, 16), (2, 16)))
    residual = bell_draw(arg_keys[1], (REP, STEPS, TOKENS, D), 1.0, 6.0, ((0, 16), (2, 16)))
    upstream = bell_draw(arg_keys[2], (REP, STEPS, TOKENS, D), 1.0, 6.0, ((0, 16), (2, 16)))
    norm_gain = jnp.clip(1.0 + 0.1 * jax.random.normal(arg_keys[3], (D,), jnp.float32), 0.5, 1.5)
    params = bell_draw(arg_keys[4], (REP, BS, OB, BPC, BS), 1.0, 6.0, ((0, 16), (1, 16)), jnp.float32)
    momentum = bell_draw(arg_keys[5], (REP, BS, OB, BPC, BS), 1.0, 6.0, ((0, 16), (1, 16)), jnp.float32)
    pattern = draw_pattern(jax.random.fold_in(arg_keys[8], 71), 0)
    step_index = jax.random.randint(arg_keys[7], (1,), 0, 3000).astype(jnp.int32)
    return dict(activations=activations, residual=residual, upstream=upstream, norm_gain=norm_gain, params=params, momentum=momentum, pattern=pattern, step_index=step_index)


learn_rate = 0.1
momentum_beta = 0.9
decay_keep = 0.999
epsilon = 1e-06

def norm_backward(pre_norm, upstream_rows, gain):
    inv_rms = lax.rsqrt(lax.optimization_barrier(jnp.mean(pre_norm * pre_norm, axis=-1, keepdims=True)) + epsilon)
    weighted = gain * upstream_rows
    inner_mean = lax.optimization_barrier(jnp.mean(pre_norm * weighted, axis=-1, keepdims=True))
    return inv_rms * weighted - pre_norm * inv_rms * inv_rms * inv_rms * inner_mean

def reference(activations, residual, upstream, norm_gain, params, momentum, pattern, step_index):
    scaling = 1.0 / math.sqrt(BPC * BS)
    gain = norm_gain.astype(jnp.float32)

    def replica_grad(inputs):
        weights, acts_rep, resid_rep, upper_rep = inputs
        low_weights = lax.optimization_barrier(weights.astype(jnp.bfloat16)).astype(jnp.float32)

        def group_term(group):
            offset = (group * TOK_DEV).astype(jnp.int32)
            acts_grp = lax.dynamic_slice_in_dim(acts_rep, offset, TOK_DEV, 0)
            resid_grp = lax.dynamic_slice_in_dim(resid_rep, offset, TOK_DEV, 0)
            upper_grp = lax.dynamic_slice_in_dim(upper_rep, offset, TOK_DEV, 0)
            picked = acts_grp.reshape(TOK_DEV, HB, BS)[:, pattern].astype(jnp.float32)
            projected = jnp.einsum('tcki,icko->tco', picked, low_weights)
            pre_norm = resid_grp.astype(jnp.float32) + scaling * projected.reshape(TOK_DEV, D)
            grad_pre = norm_backward(pre_norm, upper_grp.astype(jnp.float32), gain)
            grad_low = lax.optimization_barrier(grad_pre.astype(jnp.bfloat16)).astype(jnp.float32)
            partial_sum = jnp.einsum('tcki,tco->icko', picked, grad_low.reshape(TOK_DEV, OB, BS))
            return lax.optimization_barrier(partial_sum.astype(jnp.bfloat16)).astype(jnp.float32)
        terms = lax.map(group_term, jnp.arange(N_FSDP, dtype=jnp.int32))
        return scaling * lax.optimization_barrier(jnp.sum(terms, axis=0))
    weights_now = params
    moment = momentum
    for step_num in range(STEPS):
        gradient = lax.map(replica_grad, (weights_now, activations[:, step_num], residual[:, step_num], upstream[:, step_num]))
        moment = momentum_beta * moment + gradient
        weights_now = decay_keep * weights_now - learn_rate * moment
        hop_table = jnp.array([1, 2, 4], dtype=jnp.int32)
        hop_size = hop_table[(step_index[0] + step_num) % 3]
        partner = (jnp.arange(REP, dtype=jnp.int32) - hop_size) % REP
        weights_now = 0.5 * (weights_now + weights_now[partner])
    return (weights_now, moment)
```

```python
from functools import partial
import math

import jax
import jax.numpy as jnp
from jax import lax
from jax.experimental import pallas as pl
from jax.experimental.pallas import tpu as pltpu
from jax.sharding import PartitionSpec as P

learn_rate = 0.1
momentum_beta = 0.9
decay_keep = 0.999
epsilon = 1e-06

BF = jnp.bfloat16
F32 = jnp.float32
MESH = pl.DeviceIdType.MESH

SIDE = 4
COLS = 2
B_EVERY = 5
AG_LAG = (2, 4, 6, 8)
RS_LAG = (2, 4, 6, 8)


def mod4(v):
    return lax.rem(v + 2 * SIDE, SIDE)


def step_kernel(
    step, scaling, pat, wl, act_hbm, res_hbm, up_hbm, gain, out,
    gat, par, pre, act, act_t, res, up, ssq, spg, relay_in, first_in, last_in, last_relay,
    sems, local_sems,
):
    n_col, per_col = wl.shape[0], wl.shape[1]
    in_blocks, rows = act.shape[0], act.shape[1]
    chunks = n_col // COLS
    width = n_col * 128

    me = lax.axis_index("fsdp")
    zh, y = me // SIDE, lax.rem(me, SIDE)

    def device(z_at, y_at):
        return {"fsdp": z_at * SIDE + y_at}

    def cols(j):
        return pl.ds(j * COLS, COLS)

    def remote(src, dst, kind, j, target):
        return pltpu.make_async_remote_copy(
            src_ref=src, dst_ref=dst, send_sem=sems.at[2 * kind, j], recv_sem=sems.at[2 * kind + 1, j],
            device_id=target, device_id_type=MESH,
        )

    own = pltpu.make_async_copy(wl, gat.at[zh, y], local_sems.at[0])
    own.start()
    loads = [
        pltpu.make_async_copy(res_hbm.at[0, step], res, local_sems.at[1]),
        pltpu.make_async_copy(up_hbm.at[0, step], up, local_sems.at[2]),
    ] + [
        pltpu.make_async_copy(act_hbm.at[0, step, :, pl.ds(b * 128, 128)], act.at[b], local_sems.at[3 + b])
        for b in range(in_blocks)
    ]
    for load in loads:
        load.start()

    barrier = pltpu.get_barrier_semaphore()
    for target in (device(mod4(zh + 1), y), device(mod4(zh - 1), y), device(zh, mod4(y + 1)), device(zh, mod4(y - 1))):
        pl.semaphore_signal(barrier, inc=1, device_id=target, device_id_type=MESH)
    pl.semaphore_wait(barrier, 4)
    own.wait()

    def facts(j):
        y_first = (lax.rem(j, B_EVERY) == B_EVERY - 1).astype(jnp.int32)
        turn = 1 - 2 * lax.rem(j, 2)
        return 1 - y_first, y_first, turn

    def gather_hop1(j, way):
        z_first, y_first, _ = facts(j)
        piece = gat.at[zh, y, cols(j)]
        return remote(piece, piece, 0 if way == 1 else 1, j, device(mod4(zh + way * z_first), mod4(y + way * y_first)))

    def gather_hop1_in(j, turn):
        z_first, y_first, _ = facts(j)
        return gat.at[mod4(zh - turn * z_first), mod4(y - turn * y_first), cols(j)]

    def gather_relay1(j):
        z_first, y_first, turn = facts(j)
        piece = gather_hop1_in(j, turn)
        return remote(piece, piece, 2, j, device(mod4(zh + turn * z_first), mod4(y + turn * y_first)))

    def two_forms(j, z_form, y_form):
        z_first, _, _ = facts(j)
        pl.when(z_first == 1)(z_form)
        pl.when(z_first == 0)(y_form)

    def wait_piece(kind, j):
        piece = gat.at[zh, y, cols(j)]
        remote(piece, piece, kind, j, device(mod4(zh + 1), y)).wait_recv()

    def wait_four(kind, j):
        piece = gat.at[:, y, cols(j)]
        remote(piece, piece, kind, j, device(zh, mod4(y + 1))).wait_recv()

    def wait_by_turn(wait, j, same):
        _, _, turn = facts(j)
        forward = (turn == 1) if same else (turn == -1)
        pl.when(forward)(lambda: wait(0))
        pl.when(jnp.logical_not(forward))(lambda: wait(1))

    def g0(j):
        gather_hop1(j, 1).start()
        gather_hop1(j, -1).start()

    def g1(j):
        wait_by_turn(lambda which: wait_piece(which, j), j, True)
        gather_relay1(j).start()

    def g2(j):
        wait_by_turn(lambda which: wait_piece(which, j), j, False)
        wait_piece(2, j)

        def z_form():
            four = gat.at[:, y, cols(j)]
            remote(four, four, 3, j, device(zh, mod4(y + 1))).start()
            remote(four, four, 4, j, device(zh, mod4(y - 1))).start()

        def y_form():
            four = gat.at[zh, :, cols(j)]
            remote(four, four, 3, j, device(mod4(zh + 1), y)).start()
            remote(four, four, 4, j, device(mod4(zh - 1), y)).start()

        two_forms(j, z_form, y_form)

    def g3(j):
        wait_by_turn(lambda which: wait_four(3 + which, j), j, True)
        _, _, turn = facts(j)

        def z_form():
            four = gat.at[:, mod4(y - turn), cols(j)]
            remote(four, four, 5, j, device(zh, mod4(y + turn))).start()

        def y_form():
            four = gat.at[mod4(zh - turn), :, cols(j)]
            remote(four, four, 5, j, device(mod4(zh + turn), y)).start()

        two_forms(j, z_form, y_form)

    def picked(k):
        return pl.ds(pl.multiple_of(k * 128, 128), 128)

    def forward(c):
        lhs = jnp.concatenate([act[pat[c * per_col + k]] for k in range(per_col)], axis=1)
        rhs = jnp.concatenate(
            [gat[:, :, c, k].astype(F32).reshape(128, 128).astype(BF) for k in range(per_col)], axis=0
        )
        proj = jnp.dot(lhs, rhs, preferred_element_type=F32)
        value = res[:, picked(c)].astype(F32) + scaling * proj
        weighted = gain[pl.ds(c, 1), :] * up[:, picked(c)].astype(F32)
        pre[c] = value
        ssq[...] += value * value
        spg[...] += value * weighted

    def g4(j):
        wait_by_turn(lambda which: wait_four(3 + which, j), j, False)
        wait_four(5, j)
        for q in range(COLS):
            forward(j * COLS + q)

    ssq[...] = jnp.zeros_like(ssq)
    spg[...] = jnp.zeros_like(spg)

    def gather_step(t, carry):
        pl.when(t < chunks)(lambda: g0(t))

        @pl.when(t == 1)
        def _():
            for load in loads:
                load.wait()

        @pl.when(jnp.logical_and(t >= 1, t < 1 + in_blocks // 4))
        def _():
            for q in range(4):
                b = (t - 1) * 4 + q
                act_t[b] = act[b].astype(F32).T.astype(BF)

        for lag, stage in zip(AG_LAG, (g1, g2, g3, g4)):
            j = t - lag
            pl.when(jnp.logical_and(j >= 0, j < chunks))(lambda stage=stage, j=j: stage(j))
        return carry

    lax.fori_loop(0, chunks + AG_LAG[3], gather_step, 0)

    mean_sq = jnp.sum(ssq[...], axis=1, keepdims=True) * (1.0 / width)
    inner = jnp.sum(spg[...], axis=1, keepdims=True) * (1.0 / width)
    inv = lax.rsqrt(mean_sq + epsilon)
    ssq[...] = jnp.broadcast_to(inv, (rows, 128))
    spg[...] = jnp.broadcast_to(inv * inv * inv * inner, (rows, 128))

    def backward(c):
        weighted = gain[pl.ds(c, 1), :] * up[:, picked(c)].astype(F32)
        grad = (ssq[...] * weighted - pre[c] * spg[...]).astype(BF)
        lhs = jnp.concatenate([act_t[pat[c * per_col + k]] for k in range(per_col)], axis=0)
        result = jnp.dot(lhs, grad, preferred_element_type=F32)
        for k in range(per_col):
            par[:, :, c, k] = result[k * 128:(k + 1) * 128].reshape(SIDE, SIDE, 8, 128).astype(BF)

    def s0(j):
        for q in range(COLS):
            backward(j * COLS + q)
        _, _, turn = facts(j)

        def z_form():
            remote(par.at[:, mod4(y + 2), cols(j)], relay_in.at[:, cols(j)], 6, j, device(zh, mod4(y + turn))).start()
            remote(par.at[:, mod4(y - turn), cols(j)], first_in.at[1, :, cols(j)], 7, j, device(zh, mod4(y - turn))).start()

        def y_form():
            remote(par.at[mod4(zh + 2), :, cols(j)], relay_in.at[:, cols(j)], 6, j, device(mod4(zh + turn), y)).start()
            remote(par.at[mod4(zh - turn), :, cols(j)], first_in.at[1, :, cols(j)], 7, j, device(mod4(zh - turn), y)).start()

        two_forms(j, z_form, y_form)

    def s1(j):
        wait_four(6, j)
        _, _, turn = facts(j)

        def z_form():
            at = mod4(y + turn)
            par[:, at, cols(j)] = (par[:, at, cols(j)].astype(F32) + relay_in[:, cols(j)].astype(F32)).astype(BF)
            remote(par.at[:, at, cols(j)], first_in.at[0, :, cols(j)], 8, j, device(zh, at)).start()

        def y_form():
            at = mod4(zh + turn)
            par[at, :, cols(j)] = (par[at, :, cols(j)].astype(F32) + relay_in[:, cols(j)].astype(F32)).astype(BF)
            remote(par.at[at, :, cols(j)], first_in.at[0, :, cols(j)], 8, j, device(at, y)).start()

        two_forms(j, z_form, y_form)

    def s2(j):
        wait_four(7, j)
        wait_four(8, j)
        z_first, y_first, turn = facts(j)
        arrived = first_in[0, :, cols(j)].astype(F32) + first_in[1, :, cols(j)].astype(F32)

        def z_form():
            par[:, y, cols(j)] = (par[:, y, cols(j)].astype(F32) + arrived).astype(BF)

        def y_form():
            par[zh, :, cols(j)] = (par[zh, :, cols(j)].astype(F32) + arrived).astype(BF)

        two_forms(j, z_form, y_form)

        def place(by):
            return mod4(zh + by * z_first), mod4(y + by * y_first)

        far, back = place(2), place(-turn)
        remote(par.at[far[0], far[1], cols(j)], last_relay.at[cols(j)], 9, j, device(*place(turn))).start()
        remote(par.at[back[0], back[1], cols(j)], last_in.at[1, cols(j)], 10, j, device(*back)).start()

    def s3(j):
        wait_piece(9, j)
        z_first, y_first, turn = facts(j)
        at = mod4(zh + turn * z_first), mod4(y + turn * y_first)
        par[at[0], at[1], cols(j)] = (
            par[at[0], at[1], cols(j)].astype(F32) + last_relay[cols(j)].astype(F32)
        ).astype(BF)
        remote(par.at[at[0], at[1], cols(j)], last_in.at[0, cols(j)], 11, j, device(*at)).start()

    def s4(j):
        wait_piece(10, j)
        wait_piece(11, j)
        out[cols(j)] = (
            par[zh, y, cols(j)].astype(F32) + last_in[0, cols(j)].astype(F32) + last_in[1, cols(j)].astype(F32)
        )

    def scatter_step(t, carry):
        pl.when(t < chunks)(lambda: s0(t))
        for lag, stage in zip(RS_LAG, (s1, s2, s3, s4)):
            j = t - lag
            pl.when(jnp.logical_and(j >= 0, j < chunks))(lambda stage=stage, j=j: stage(j))
        return carry

    lax.fori_loop(0, chunks + RS_LAG[3], scatter_step, 0)

    def finish(j, carry):
        piece, four = gat.at[zh, y, cols(j)], gat.at[:, y, cols(j)]
        for kind, ref in ((0, piece), (1, piece), (2, piece), (3, four), (4, four), (5, four),
                          (6, four), (7, four), (8, four), (9, piece), (10, piece), (11, piece)):
            remote(ref, ref, kind, j, device(mod4(zh + 1), y)).wait_send()
        return carry

    lax.fori_loop(0, chunks, finish, 0)


def gradient_of(step, low_weights, activations, residual, upstream, norm_gain, pattern):
    n_col, per_col = pattern.shape
    rows, features = activations.shape[2], activations.shape[3]
    width = residual.shape[3]
    chunks = n_col // COLS
    scaling = 1.0 / math.sqrt(per_col * 128)
    piece = (n_col, per_col, 8, 128)
    vmem, hbm, smem = pltpu.VMEM, pl.ANY, pltpu.SMEM
    return pl.pallas_call(
        partial(step_kernel, step, scaling),
        out_shape=jax.ShapeDtypeStruct(piece, F32),
        in_specs=[
            pl.BlockSpec(memory_space=smem),
            pl.BlockSpec(memory_space=hbm),
            pl.BlockSpec(memory_space=hbm),
            pl.BlockSpec(memory_space=hbm),
            pl.BlockSpec(memory_space=hbm),
            pl.BlockSpec(memory_space=vmem),
        ],
        out_specs=pl.BlockSpec(memory_space=vmem),
        scratch_shapes=[
            vmem((SIDE, SIDE) + piece, BF),
            vmem((SIDE, SIDE) + piece, BF),
            vmem((n_col, rows, 128), F32),
            vmem((features // 128, rows, 128), BF),
            vmem((features // 128, 128, rows), BF),
            vmem((rows, width), BF),
            vmem((rows, width), BF),
            vmem((rows, 128), F32),
            vmem((rows, 128), F32),
            vmem((SIDE,) + piece, BF),
            vmem((2, SIDE) + piece, BF),
            vmem((2,) + piece, BF),
            vmem(piece, BF),
            pltpu.SemaphoreType.DMA((24, chunks)),
            pltpu.SemaphoreType.DMA((3 + features // 128,)),
        ],
        compiler_params=pltpu.CompilerParams(
            collective_id=step, has_side_effects=True, vmem_limit_bytes=60 * 1024 * 1024
        ),
        name="step",
    )(pattern.reshape(-1), low_weights, activations, residual, upstream, norm_gain.reshape(n_col, 128))


def gossip(weights, stride):
    devices = lax.axis_size("rep")
    stride = stride % devices
    if stride == 0:
        return weights
    partner = lax.ppermute(weights.astype(BF), "rep", [(i, (i + stride) % devices) for i in range(devices)])
    return 0.5 * (weights + partner.astype(F32))


def body(activations, residual, upstream, norm_gain, params, momentum, pattern, step_index):
    per_col = pattern.shape[1]
    scaling = 1.0 / math.sqrt(per_col * 128)
    weights_now = params
    moment = momentum
    for step_num in range(activations.shape[1]):
        low_weights = weights_now[0].astype(BF).transpose(1, 2, 0, 3)
        total = gradient_of(step_num, low_weights, activations, residual, upstream, norm_gain, pattern)
        gradient = total.transpose(2, 0, 1, 3)
        moment = momentum_beta * moment + (scaling * gradient)[None]
        weights_now = decay_keep * weights_now - learn_rate * moment
        branches = [partial(gossip, stride=1), partial(gossip, stride=2), partial(gossip, stride=4)]
        weights_now = lax.switch((step_index[0] + step_num) % 3, branches, weights_now)
    return (weights_now, moment)


def solution(mesh):
    in_specs = (
        P("rep", None, "fsdp", None),
        P("rep", None, "fsdp", None),
        P("rep", None, "fsdp", None),
        P(),
        P("rep", "fsdp", None, None, None),
        P("rep", "fsdp", None, None, None),
        P(),
        P(),
    )
    out_specs = (P("rep", "fsdp", None, None, None), P("rep", "fsdp", None, None, None))
    return jax.shard_map(body, mesh=mesh, in_specs=in_specs, out_specs=out_specs, check_vma=False)
```

```python
from functools import partial
import math

import jax
import jax.numpy as jnp
from jax import lax
from jax.experimental import pallas as pl
from jax.experimental.pallas import tpu as pltpu
from jax.sharding import PartitionSpec as P

learn_rate = 0.1
momentum_beta = 0.9
decay_keep = 0.999
epsilon = 1e-06

BF = jnp.bfloat16
F32 = jnp.float32
MESH = pl.DeviceIdType.MESH

SIDE = 4
COLS = 2
B_EVERY = 5
AG_LAG = (3, 6, 9, 12)
RS_LAG = (3, 6, 9, 12)
HOP_LAG = 2
STEPS = 2


def mod4(v):
    return lax.rem(v + 2 * SIDE, SIDE)


def steps_kernel(
    hops, scaling, pat, w_in, m_in, act_hbm, res_hbm, up_hbm, gain, w_out, m_out,
    gat, par, pre, act, act_t, res, up, ssq, spg, relay_in, first_in, last_in, last_relay, hop_out, hop_in,
    sems, local_sems,
):
    n_col, per_col = w_in.shape[0], w_in.shape[1]
    in_blocks, rows = act.shape[1], act.shape[2]
    chunks = n_col // COLS
    width = n_col * 128
    replicas = lax.axis_size("rep")

    rep = lax.axis_index("rep")
    me = lax.axis_index("fsdp")
    zh, y = me // SIDE, lax.rem(me, SIDE)

    def device(z_at, y_at):
        return {"fsdp": z_at * SIDE + y_at}

    def cols(j):
        return pl.ds(j * COLS, COLS)

    def remote(src, dst, kind, j, target):
        return pltpu.make_async_remote_copy(
            src_ref=src, dst_ref=dst, send_sem=sems.at[2 * kind, j], recv_sem=sems.at[2 * kind + 1, j],
            device_id=target, device_id_type=MESH,
        )

    def loads(s):
        at = s * (2 + in_blocks)
        return [
            pltpu.make_async_copy(res_hbm.at[0, s], res.at[s], local_sems.at[at]),
            pltpu.make_async_copy(up_hbm.at[0, s], up.at[s], local_sems.at[at + 1]),
        ] + [
            pltpu.make_async_copy(act_hbm.at[0, s, :, pl.ds(b * 128, 128)], act.at[s, b], local_sems.at[at + 2 + b])
            for b in range(in_blocks)
        ]

    for load in loads(0):
        load.start()

    barrier = pltpu.get_barrier_semaphore()
    targets = [device(mod4(zh + 1), y), device(mod4(zh - 1), y), device(zh, mod4(y + 1)), device(zh, mod4(y - 1))]
    for hop in hops:
        targets += [{"rep": lax.rem(rep + hop, replicas)}, {"rep": lax.rem(rep + replicas - hop, replicas)}]
    for target in targets:
        pl.semaphore_signal(barrier, inc=1, device_id=target, device_id_type=MESH)
    gat[zh, y] = w_in[...].astype(BF)
    ssq[...] = jnp.zeros_like(ssq)
    spg[...] = jnp.zeros_like(spg)
    pl.semaphore_wait(barrier, len(targets))

    def facts(j):
        y_first = (lax.rem(j, B_EVERY) == B_EVERY - 1).astype(jnp.int32)
        turn = 1 - 2 * lax.rem(j, 2)
        return 1 - y_first, y_first, turn

    def two_forms(j, z_form, y_form):
        z_first, _, _ = facts(j)
        pl.when(z_first == 1)(z_form)
        pl.when(z_first == 0)(y_form)

    def piece_copy(kind, j):
        piece = gat.at[zh, y, cols(j)]
        return remote(piece, piece, kind, j, device(mod4(zh + 1), y))

    def four_copy(kind, j):
        four = gat.at[:, y, cols(j)]
        return remote(four, four, kind, j, device(zh, mod4(y + 1)))

    def wait_by_turn(copy, kind, j, same):
        _, _, turn = facts(j)
        forward = (turn == 1) if same else (turn == -1)
        pl.when(forward)(lambda: copy(kind, j).wait_recv())
        pl.when(jnp.logical_not(forward))(lambda: copy(kind + 1, j).wait_recv())

    def g0(s, j):
        z_first, y_first, _ = facts(j)
        piece = gat.at[zh, y, cols(j)]
        for kind, way in ((0, 1), (1, -1)):
            remote(piece, piece, kind, j, device(mod4(zh + way * z_first), mod4(y + way * y_first))).start()

    def g1(s, j):
        wait_by_turn(piece_copy, 0, j, True)
        z_first, y_first, turn = facts(j)
        piece = gat.at[mod4(zh - turn * z_first), mod4(y - turn * y_first), cols(j)]
        remote(piece, piece, 2, j, device(mod4(zh + turn * z_first), mod4(y + turn * y_first))).start()

    def g2(s, j):
        wait_by_turn(piece_copy, 0, j, False)
        piece_copy(2, j).wait_recv()

        def z_form():
            four = gat.at[:, y, cols(j)]
            remote(four, four, 3, j, device(zh, mod4(y + 1))).start()
            remote(four, four, 4, j, device(zh, mod4(y - 1))).start()

        def y_form():
            four = gat.at[zh, :, cols(j)]
            remote(four, four, 3, j, device(mod4(zh + 1), y)).start()
            remote(four, four, 4, j, device(mod4(zh - 1), y)).start()

        two_forms(j, z_form, y_form)

    def g3(s, j):
        wait_by_turn(four_copy, 3, j, True)
        _, _, turn = facts(j)

        def z_form():
            four = gat.at[:, mod4(y - turn), cols(j)]
            remote(four, four, 5, j, device(zh, mod4(y + turn))).start()

        def y_form():
            four = gat.at[mod4(zh - turn), :, cols(j)]
            remote(four, four, 5, j, device(mod4(zh + turn), y)).start()

        two_forms(j, z_form, y_form)

    def lanes(c):
        return pl.ds(pl.multiple_of(c * 128, 128), 128)

    def forward(s, c):
        lhs = jnp.concatenate([act[s, pat[c * per_col + k]] for k in range(per_col)], axis=1)
        rhs = jnp.concatenate(
            [gat[:, :, c, k].astype(F32).reshape(128, 128).astype(BF) for k in range(per_col)], axis=0
        )
        proj = jnp.dot(lhs, rhs, preferred_element_type=F32)
        value = res[s, :, lanes(c)].astype(F32) + scaling * proj
        weighted = gain[pl.ds(c, 1), :] * up[s, :, lanes(c)].astype(F32)
        pre[c] = value
        ssq[s] += value * value
        spg[s] += value * weighted

    def g4(s, j):
        wait_by_turn(four_copy, 3, j, False)
        four_copy(5, j).wait_recv()
        for q in range(COLS):
            forward(s, j * COLS + q)
        for kind in range(3):
            piece_copy(kind, j).wait_send()
            four_copy(3 + kind, j).wait_send()

    def norm(s):
        inv = lax.rsqrt(jnp.sum(ssq[s], axis=1, keepdims=True) * (1.0 / width) + epsilon)
        inner = jnp.sum(spg[s], axis=1, keepdims=True) * (1.0 / width)
        ssq[s] = jnp.broadcast_to(inv, (rows, 128))
        spg[s] = jnp.broadcast_to(inv * inv * inv * inner, (rows, 128))

    def backward(s, c):
        weighted = gain[pl.ds(c, 1), :] * up[s, :, lanes(c)].astype(F32)
        grad = (ssq[s] * weighted - pre[c] * spg[s]).astype(BF)
        lhs = jnp.concatenate([act_t[s, pat[c * per_col + k]] for k in range(per_col)], axis=0)
        result = jnp.dot(lhs, grad, preferred_element_type=F32)
        for k in range(per_col):
            par[:, :, c, k] = result[k * 128:(k + 1) * 128].reshape(SIDE, SIDE, 8, 128).astype(BF)

    def s0(s, j):
        for q in range(COLS):
            backward(s, j * COLS + q)
        _, _, turn = facts(j)

        def z_form():
            remote(par.at[:, mod4(y + 2), cols(j)], relay_in.at[:, cols(j)], 6, j, device(zh, mod4(y + turn))).start()
            remote(par.at[:, mod4(y - turn), cols(j)], first_in.at[1, :, cols(j)], 7, j, device(zh, mod4(y - turn))).start()

        def y_form():
            remote(par.at[mod4(zh + 2), :, cols(j)], relay_in.at[:, cols(j)], 6, j, device(mod4(zh + turn), y)).start()
            remote(par.at[mod4(zh - turn), :, cols(j)], first_in.at[1, :, cols(j)], 7, j, device(mod4(zh - turn), y)).start()

        two_forms(j, z_form, y_form)

    def s1(s, j):
        four_copy(6, j).wait_recv()
        _, _, turn = facts(j)

        def z_form():
            at = mod4(y + turn)
            par[:, at, cols(j)] = (par[:, at, cols(j)].astype(F32) + relay_in[:, cols(j)].astype(F32)).astype(BF)
            remote(par.at[:, at, cols(j)], first_in.at[0, :, cols(j)], 8, j, device(zh, at)).start()

        def y_form():
            at = mod4(zh + turn)
            par[at, :, cols(j)] = (par[at, :, cols(j)].astype(F32) + relay_in[:, cols(j)].astype(F32)).astype(BF)
            remote(par.at[at, :, cols(j)], first_in.at[0, :, cols(j)], 8, j, device(at, y)).start()

        two_forms(j, z_form, y_form)

    def s2(s, j):
        four_copy(7, j).wait_recv()
        four_copy(8, j).wait_recv()
        z_first, y_first, turn = facts(j)
        arrived = first_in[0, :, cols(j)].astype(F32) + first_in[1, :, cols(j)].astype(F32)

        def z_form():
            par[:, y, cols(j)] = (par[:, y, cols(j)].astype(F32) + arrived).astype(BF)

        def y_form():
            par[zh, :, cols(j)] = (par[zh, :, cols(j)].astype(F32) + arrived).astype(BF)

        two_forms(j, z_form, y_form)

        def place(by):
            return mod4(zh + by * z_first), mod4(y + by * y_first)

        far, back = place(2), place(-turn)
        remote(par.at[far[0], far[1], cols(j)], last_relay.at[cols(j)], 9, j, device(*place(turn))).start()
        remote(par.at[back[0], back[1], cols(j)], last_in.at[1, cols(j)], 10, j, device(*back)).start()

    def s3(s, j):
        piece_copy(9, j).wait_recv()
        z_first, y_first, turn = facts(j)
        at = mod4(zh + turn * z_first), mod4(y + turn * y_first)
        par[at[0], at[1], cols(j)] = (
            par[at[0], at[1], cols(j)].astype(F32) + last_relay[cols(j)].astype(F32)
        ).astype(BF)
        remote(par.at[at[0], at[1], cols(j)], last_in.at[0, cols(j)], 11, j, device(*at)).start()

    def hop_copy(s, j):
        hop = hops[0] + s * (hops[1] - hops[0])
        return remote(hop_out.at[cols(j)], hop_in.at[s, cols(j)], 12 + s, j, {"rep": lax.rem(rep + hop, replicas)})

    def s4(s, j):
        piece_copy(10, j).wait_recv()
        piece_copy(11, j).wait_recv()
        total = (
            par[zh, y, cols(j)].astype(F32) + last_in[0, cols(j)].astype(F32) + last_in[1, cols(j)].astype(F32)
        )
        moment = momentum_beta * m_out[cols(j)] + scaling * total
        weights = decay_keep * w_out[cols(j)] - learn_rate * moment
        m_out[cols(j)] = moment
        w_out[cols(j)] = weights
        hop_out[cols(j)] = weights.astype(BF)
        hop_copy(s, j).start()

    def s5(s, j):
        hop_copy(s, j).wait()
        weights = 0.5 * (w_out[cols(j)] + hop_in[s, cols(j)].astype(F32))
        w_out[cols(j)] = weights

        @pl.when(s == 0)
        def _():
            gat[zh, y, cols(j)] = weights.astype(BF)
            g0(s, j)

        for kind in range(3):
            four_copy(6 + kind, j).wait_send()
            piece_copy(9 + kind, j).wait_send()

    w_out[...] = w_in[...]
    m_out[...] = m_in[...]

    scatter_from = chunks + AG_LAG[3]
    next_gather = scatter_from + RS_LAG[3] + HOP_LAG
    scatter_again = next_gather + scatter_from
    last = scatter_again + chunks + RS_LAG[3] + HOP_LAG

    def run(stage, t, start, period):
        since = t - start
        s = (since >= period).astype(jnp.int32)
        j = since - s * period
        pl.when(jnp.logical_and(j >= 0, j < chunks))(lambda: stage(s, j))

    def iteration(t, carry):
        pl.when(t < chunks)(lambda: g0(0, t))

        @pl.when(t == 1)
        def _():
            for load in loads(0):
                load.wait()
            for load in loads(1):
                load.start()

        @pl.when(t == chunks // 2)
        def _():
            for load in loads(1):
                load.wait()

        for s, start in ((0, 1), (1, chunks // 2)):
            @pl.when(jnp.logical_and(t >= start, t < start + in_blocks // 4))
            def _(s=s, start=start):
                for q in range(4):
                    b = (t - start) * 4 + q
                    act_t[s, b] = act[s, b].astype(F32).T.astype(BF)

        for lag, stage in zip(RS_LAG + (RS_LAG[3] + HOP_LAG,), (s1, s2, s3, s4, s5)):
            run(stage, t, scatter_from + lag, scatter_again - scatter_from)
        run(s0, t, scatter_from, scatter_again - scatter_from)
        for lag, stage in zip(AG_LAG, (g1, g2, g3, g4)):
            run(stage, t, lag, next_gather)

        for s, at in ((0, scatter_from - 1), (1, scatter_again - 1)):
            pl.when(t == at)(lambda s=s: norm(s))
        return carry

    lax.fori_loop(0, last, iteration, 0)


def two_steps(number, hops, weights, moment, activations, residual, upstream, norm_gain, pattern):
    n_col, per_col = pattern.shape
    steps, rows, features = activations.shape[1:]
    width = residual.shape[3]
    chunks = n_col // COLS
    in_blocks = features // 128
    scaling = 1.0 / math.sqrt(per_col * 128)
    piece = (n_col, per_col, 8, 128)
    vmem, hbm, smem = pltpu.VMEM, pl.ANY, pltpu.SMEM
    return pl.pallas_call(
        partial(steps_kernel, hops, scaling),
        out_shape=[jax.ShapeDtypeStruct(piece, F32)] * 2,
        in_specs=[
            pl.BlockSpec(memory_space=smem),
            pl.BlockSpec(memory_space=vmem),
            pl.BlockSpec(memory_space=vmem),
            pl.BlockSpec(memory_space=hbm),
            pl.BlockSpec(memory_space=hbm),
            pl.BlockSpec(memory_space=hbm),
            pl.BlockSpec(memory_space=vmem),
        ],
        out_specs=[pl.BlockSpec(memory_space=vmem)] * 2,
        scratch_shapes=[
            vmem((SIDE, SIDE) + piece, BF),
            vmem((SIDE, SIDE) + piece, BF),
            vmem((n_col, rows, 128), F32),
            vmem((steps, in_blocks, rows, 128), BF),
            vmem((steps, in_blocks, 128, rows), BF),
            vmem((steps, rows, width), BF),
            vmem((steps, rows, width), BF),
            vmem((steps, rows, 128), F32),
            vmem((steps, rows, 128), F32),
            vmem((SIDE,) + piece, BF),
            vmem((2, SIDE) + piece, BF),
            vmem((2,) + piece, BF),
            vmem(piece, BF),
            vmem(piece, BF),
            vmem((steps,) + piece, BF),
            pltpu.SemaphoreType.DMA((2 * (12 + steps), chunks)),
            pltpu.SemaphoreType.DMA((steps * (2 + in_blocks),)),
        ],
        compiler_params=pltpu.CompilerParams(
            collective_id=number, has_side_effects=True, vmem_limit_bytes=60 * 1024 * 1024
        ),
        name="two_steps",
    )(pattern.reshape(-1), weights, moment, activations, residual, upstream, norm_gain.reshape(n_col, 128))


def body(activations, residual, upstream, norm_gain, params, momentum, pattern, step_index):
    weights, moment = (a[0].transpose(1, 2, 0, 3) for a in (params, momentum))
    hops = [1, 2, 4]
    branches = [
        partial(two_steps, first, (hops[first], hops[(first + 1) % 3])) for first in range(3)
    ]
    weights, moment = lax.switch(
        step_index[0] % 3, branches, weights, moment, activations, residual, upstream, norm_gain, pattern
    )
    return tuple(a.transpose(2, 0, 1, 3)[None] for a in (weights, moment))


def solution(mesh):
    in_specs = (
        P("rep", None, "fsdp", None),
        P("rep", None, "fsdp", None),
        P("rep", None, "fsdp", None),
        P(),
        P("rep", "fsdp", None, None, None),
        P("rep", "fsdp", None, None, None),
        P(),
        P(),
    )
    out_specs = (P("rep", "fsdp", None, None, None), P("rep", "fsdp", None, None, None))
    return jax.shard_map(body, mesh=mesh, in_specs=in_specs, out_specs=out_specs, check_vma=False)
```

```python
from functools import partial
import math

import jax
import jax.numpy as jnp
from jax import lax
from jax.experimental import pallas as pl
from jax.experimental.pallas import tpu as pltpu
from jax.sharding import PartitionSpec as P

learn_rate = 0.1
momentum_beta = 0.9
decay_keep = 0.999
epsilon = 1e-06

BF = jnp.bfloat16
F32 = jnp.float32
MESH = pl.DeviceIdType.MESH

SIDE = 4
COLS = 2
B_EVERY = 5
AG_LAG = (3, 6, 9, 12)
RS_LAG = (3, 6, 9, 12)
HOP_LAG = 2
STEPS = 2


def mod4(v):
    return lax.rem(v + 2 * SIDE, SIDE)


def steps_kernel(
    hops, scaling, pat, w_in, m_in, act_hbm, res_hbm, up_hbm, gain, w_out, m_out,
    gat, par, pre, act, act_t, res, up, ssq, spg, relay_in, first_in, last_in, last_relay, hop_out, hop_in,
    sems, local_sems,
):
    n_col, per_col = w_in.shape[0], w_in.shape[1]
    in_blocks, rows = act.shape[1], act.shape[2]
    chunks = n_col // COLS
    width = n_col * 128
    replicas = lax.axis_size("rep")

    rep = lax.axis_index("rep")
    me = lax.axis_index("fsdp")
    zh, y = me // SIDE, lax.rem(me, SIDE)

    def device(z_at, y_at):
        return {"fsdp": z_at * SIDE + y_at}

    def cols(j):
        return pl.ds(j * COLS, COLS)

    def remote(src, dst, kind, j, target):
        return pltpu.make_async_remote_copy(
            src_ref=src, dst_ref=dst, send_sem=sems.at[2 * kind, j], recv_sem=sems.at[2 * kind + 1, j],
            device_id=target, device_id_type=MESH,
        )

    def loads(s):
        at = s * (2 + in_blocks)
        return [
            pltpu.make_async_copy(res_hbm.at[0, s], res.at[s], local_sems.at[at]),
            pltpu.make_async_copy(up_hbm.at[0, s], up.at[s], local_sems.at[at + 1]),
        ] + [
            pltpu.make_async_copy(act_hbm.at[0, s, :, pl.ds(b * 128, 128)], act.at[s, b], local_sems.at[at + 2 + b])
            for b in range(in_blocks)
        ]

    for load in loads(0):
        load.start()

    barrier = pltpu.get_barrier_semaphore()
    targets = [device(mod4(zh + 1), y), device(mod4(zh - 1), y), device(zh, mod4(y + 1)), device(zh, mod4(y - 1))]
    for hop in hops:
        targets += [{"rep": lax.rem(rep + hop, replicas)}, {"rep": lax.rem(rep + replicas - hop, replicas)}]
    for target in targets:
        pl.semaphore_signal(barrier, inc=1, device_id=target, device_id_type=MESH)
    gat[zh, y] = w_in[...].astype(BF)
    ssq[...] = jnp.zeros_like(ssq)
    spg[...] = jnp.zeros_like(spg)
    pl.semaphore_wait(barrier, len(targets))

    def facts(j):
        y_first = (lax.rem(j, B_EVERY) == B_EVERY - 1).astype(jnp.int32)
        turn = 1 - 2 * lax.rem(j, 2)
        return 1 - y_first, y_first, turn

    def two_forms(j, z_form, y_form):
        z_first, _, _ = facts(j)
        pl.when(z_first == 1)(z_form)
        pl.when(z_first == 0)(y_form)

    def piece_copy(kind, j):
        piece = gat.at[zh, y, cols(j)]
        return remote(piece, piece, kind, j, device(mod4(zh + 1), y))

    def four_copy(kind, j):
        four = gat.at[:, y, cols(j)]
        return remote(four, four, kind, j, device(zh, mod4(y + 1)))

    def wait_by_turn(copy, kind, j, same):
        _, _, turn = facts(j)
        forward = (turn == 1) if same else (turn == -1)
        pl.when(forward)(lambda: copy(kind, j).wait_recv())
        pl.when(jnp.logical_not(forward))(lambda: copy(kind + 1, j).wait_recv())

    def g0(s, j):
        z_first, y_first, _ = facts(j)
        piece = gat.at[zh, y, cols(j)]
        for kind, way in ((0, 1), (1, -1)):
            remote(piece, piece, kind, j, device(mod4(zh + way * z_first), mod4(y + way * y_first))).start()

    def g1(s, j):
        wait_by_turn(piece_copy, 0, j, True)
        z_first, y_first, turn = facts(j)
        piece = gat.at[mod4(zh - turn * z_first), mod4(y - turn * y_first), cols(j)]
        remote(piece, piece, 2, j, device(mod4(zh + turn * z_first), mod4(y + turn * y_first))).start()

    def g2(s, j):
        wait_by_turn(piece_copy, 0, j, False)
        piece_copy(2, j).wait_recv()

        def z_form():
            four = gat.at[:, y, cols(j)]
            remote(four, four, 3, j, device(zh, mod4(y + 1))).start()
            remote(four, four, 4, j, device(zh, mod4(y - 1))).start()

        def y_form():
            four = gat.at[zh, :, cols(j)]
            remote(four, four, 3, j, device(mod4(zh + 1), y)).start()
            remote(four, four, 4, j, device(mod4(zh - 1), y)).start()

        two_forms(j, z_form, y_form)

    def g3(s, j):
        wait_by_turn(four_copy, 3, j, True)
        _, _, turn = facts(j)

        def z_form():
            four = gat.at[:, mod4(y - turn), cols(j)]
            remote(four, four, 5, j, device(zh, mod4(y + turn))).start()

        def y_form():
            four = gat.at[mod4(zh - turn), :, cols(j)]
            remote(four, four, 5, j, device(mod4(zh + turn), y)).start()

        two_forms(j, z_form, y_form)

    def lanes(c):
        return pl.ds(pl.multiple_of(c * 128, 128), 128)

    def forward(s, c):
        lhs = jnp.concatenate([act[s, pat[k, c]] for k in range(per_col)], axis=1)
        rhs = jnp.concatenate(
            [gat[:, :, c, k].astype(F32).reshape(128, 128).astype(BF) for k in range(per_col)], axis=0
        )
        proj = jnp.dot(lhs, rhs, preferred_element_type=F32)
        value = res[s, :, lanes(c)].astype(F32) + scaling * proj
        weighted = gain[pl.ds(c, 1), :] * up[s, :, lanes(c)].astype(F32)
        pre[c] = value
        ssq[s] += value * value
        spg[s] += value * weighted

    def g4(s, j):
        wait_by_turn(four_copy, 3, j, False)
        four_copy(5, j).wait_recv()
        for q in range(COLS):
            forward(s, j * COLS + q)
        for kind in range(3):
            piece_copy(kind, j).wait_send()
            four_copy(3 + kind, j).wait_send()

    def norm(s):
        inv = lax.rsqrt(jnp.sum(ssq[s], axis=1, keepdims=True) * (1.0 / width) + epsilon)
        inner = jnp.sum(spg[s], axis=1, keepdims=True) * (1.0 / width)
        ssq[s] = jnp.broadcast_to(inv, (rows, 128))
        spg[s] = jnp.broadcast_to(inv * inv * inv * inner, (rows, 128))

    def backward(s, c):
        weighted = gain[pl.ds(c, 1), :] * up[s, :, lanes(c)].astype(F32)
        grad = (ssq[s] * weighted - pre[c] * spg[s]).astype(BF)
        lhs = jnp.concatenate([act_t[s, pat[k, c]] for k in range(per_col)], axis=0)
        result = jnp.dot(lhs, grad, preferred_element_type=F32)
        for k in range(per_col):
            par[:, :, c, k] = result[k * 128:(k + 1) * 128].reshape(SIDE, SIDE, 8, 128).astype(BF)

    def s0(s, j):
        for q in range(COLS):
            backward(s, j * COLS + q)
        _, _, turn = facts(j)

        def z_form():
            remote(par.at[:, mod4(y + 2), cols(j)], relay_in.at[:, cols(j)], 6, j, device(zh, mod4(y + turn))).start()
            remote(par.at[:, mod4(y - turn), cols(j)], first_in.at[1, :, cols(j)], 7, j, device(zh, mod4(y - turn))).start()

        def y_form():
            remote(par.at[mod4(zh + 2), :, cols(j)], relay_in.at[:, cols(j)], 6, j, device(mod4(zh + turn), y)).start()
            remote(par.at[mod4(zh - turn), :, cols(j)], first_in.at[1, :, cols(j)], 7, j, device(mod4(zh - turn), y)).start()

        two_forms(j, z_form, y_form)

    def s1(s, j):
        four_copy(6, j).wait_recv()
        _, _, turn = facts(j)

        def z_form():
            at = mod4(y + turn)
            par[:, at, cols(j)] = (par[:, at, cols(j)].astype(F32) + relay_in[:, cols(j)].astype(F32)).astype(BF)
            remote(par.at[:, at, cols(j)], first_in.at[0, :, cols(j)], 8, j, device(zh, at)).start()

        def y_form():
            at = mod4(zh + turn)
            par[at, :, cols(j)] = (par[at, :, cols(j)].astype(F32) + relay_in[:, cols(j)].astype(F32)).astype(BF)
            remote(par.at[at, :, cols(j)], first_in.at[0, :, cols(j)], 8, j, device(at, y)).start()

        two_forms(j, z_form, y_form)

    def s2(s, j):
        four_copy(7, j).wait_recv()
        four_copy(8, j).wait_recv()
        z_first, y_first, turn = facts(j)
        arrived = first_in[0, :, cols(j)].astype(F32) + first_in[1, :, cols(j)].astype(F32)

        def z_form():
            par[:, y, cols(j)] = (par[:, y, cols(j)].astype(F32) + arrived).astype(BF)

        def y_form():
            par[zh, :, cols(j)] = (par[zh, :, cols(j)].astype(F32) + arrived).astype(BF)

        two_forms(j, z_form, y_form)

        def place(by):
            return mod4(zh + by * z_first), mod4(y + by * y_first)

        far, back = place(2), place(-turn)
        remote(par.at[far[0], far[1], cols(j)], last_relay.at[cols(j)], 9, j, device(*place(turn))).start()
        remote(par.at[back[0], back[1], cols(j)], last_in.at[1, cols(j)], 10, j, device(*back)).start()

    def s3(s, j):
        piece_copy(9, j).wait_recv()
        z_first, y_first, turn = facts(j)
        at = mod4(zh + turn * z_first), mod4(y + turn * y_first)
        par[at[0], at[1], cols(j)] = (
            par[at[0], at[1], cols(j)].astype(F32) + last_relay[cols(j)].astype(F32)
        ).astype(BF)
        remote(par.at[at[0], at[1], cols(j)], last_in.at[0, cols(j)], 11, j, device(*at)).start()

    def hop_copy(s, j):
        hop = hops[0] + s * (hops[1] - hops[0])
        return remote(hop_out.at[cols(j)], hop_in.at[s, cols(j)], 12 + s, j, {"rep": lax.rem(rep + hop, replicas)})

    def s4(s, j):
        piece_copy(10, j).wait_recv()
        piece_copy(11, j).wait_recv()
        total = (
            par[zh, y, cols(j)].astype(F32) + last_in[0, cols(j)].astype(F32) + last_in[1, cols(j)].astype(F32)
        )
        moment = momentum_beta * m_out[cols(j)] + scaling * total
        weights = decay_keep * w_out[cols(j)] - learn_rate * moment
        m_out[cols(j)] = moment
        w_out[cols(j)] = weights
        hop_out[cols(j)] = weights.astype(BF)
        hop_copy(s, j).start()

    def s5(s, j):
        hop_copy(s, j).wait()
        weights = 0.5 * (w_out[cols(j)] + hop_in[s, cols(j)].astype(F32))
        w_out[cols(j)] = weights

        @pl.when(s == 0)
        def _():
            gat[zh, y, cols(j)] = weights.astype(BF)
            g0(s, j)

        for kind in range(3):
            four_copy(6 + kind, j).wait_send()
            piece_copy(9 + kind, j).wait_send()

    scatter_from = chunks + AG_LAG[3]
    next_gather = scatter_from + RS_LAG[3] + HOP_LAG
    scatter_again = next_gather + scatter_from
    last = scatter_again + chunks + RS_LAG[3] + HOP_LAG

    def run(stage, t, start, period):
        since = t - start
        s = (since >= period).astype(jnp.int32)
        j = since - s * period
        pl.when(jnp.logical_and(j >= 0, j < chunks))(lambda: stage(s, j))

    def iteration(t, carry):
        pl.when(t < chunks)(lambda: g0(0, t))

        @pl.when(t == 2)
        def _():
            w_out[...] = w_in[...]
            m_out[...] = m_in[...]

        @pl.when(t == 5)
        def _():
            for load in loads(0):
                load.wait()
            for load in loads(1):
                load.start()

        @pl.when(t == chunks // 2)
        def _():
            for load in loads(1):
                load.wait()

        for s, start in ((0, 5), (1, chunks // 2)):
            @pl.when(jnp.logical_and(t >= start, t < start + in_blocks // 4))
            def _(s=s, start=start):
                for q in range(4):
                    b = (t - start) * 4 + q
                    act_t[s, b] = act[s, b].astype(F32).T.astype(BF)

        for lag, stage in zip(RS_LAG + (RS_LAG[3] + HOP_LAG,), (s1, s2, s3, s4, s5)):
            run(stage, t, scatter_from + lag, scatter_again - scatter_from)
        run(s0, t, scatter_from, scatter_again - scatter_from)
        for lag, stage in zip(AG_LAG, (g1, g2, g3, g4)):
            run(stage, t, lag, next_gather)

        for s, at in ((0, scatter_from - 1), (1, scatter_again - 1)):
            pl.when(t == at)(lambda s=s: norm(s))
        return carry

    lax.fori_loop(0, last, iteration, 0)


def two_steps(number, hops, weights, moment, activations, residual, upstream, norm_gain, pattern):
    n_col, per_col = pattern.shape
    steps, rows, features = activations.shape[1:]
    width = residual.shape[3]
    chunks = n_col // COLS
    in_blocks = features // 128
    scaling = 1.0 / math.sqrt(per_col * 128)
    piece = (n_col, per_col, 8, 128)
    vmem, hbm, smem = pltpu.VMEM, pl.ANY, pltpu.SMEM
    return pl.pallas_call(
        partial(steps_kernel, hops, scaling),
        out_shape=[jax.ShapeDtypeStruct(piece, F32)] * 2,
        in_specs=[
            pl.BlockSpec(memory_space=smem),
            pl.BlockSpec(memory_space=vmem),
            pl.BlockSpec(memory_space=vmem),
            pl.BlockSpec(memory_space=hbm),
            pl.BlockSpec(memory_space=hbm),
            pl.BlockSpec(memory_space=hbm),
            pl.BlockSpec(memory_space=vmem),
        ],
        out_specs=[pl.BlockSpec(memory_space=vmem)] * 2,
        scratch_shapes=[
            vmem((SIDE, SIDE) + piece, BF),
            vmem((SIDE, SIDE) + piece, BF),
            vmem((n_col, rows, 128), F32),
            vmem((steps, in_blocks, rows, 128), BF),
            vmem((steps, in_blocks, 128, rows), BF),
            vmem((steps, rows, width), BF),
            vmem((steps, rows, width), BF),
            vmem((steps, rows, 128), F32),
            vmem((steps, rows, 128), F32),
            vmem((SIDE,) + piece, BF),
            vmem((2, SIDE) + piece, BF),
            vmem((2,) + piece, BF),
            vmem(piece, BF),
            vmem(piece, BF),
            vmem((steps,) + piece, BF),
            pltpu.SemaphoreType.DMA((2 * (12 + steps), chunks)),
            pltpu.SemaphoreType.DMA((steps * (2 + in_blocks),)),
        ],
        compiler_params=pltpu.CompilerParams(
            collective_id=number, has_side_effects=True, vmem_limit_bytes=60 * 1024 * 1024
        ),
        name="two_steps",
    )(pattern.T, weights, moment, activations, residual, upstream, norm_gain.reshape(n_col, 128))


def body(activations, residual, upstream, norm_gain, params, momentum, pattern, step_index):
    weights, moment = (a[0].transpose(1, 2, 0, 3) for a in (params, momentum))
    hops = [1, 2, 4]
    branches = [
        partial(two_steps, first, (hops[first], hops[(first + 1) % 3])) for first in range(3)
    ]
    weights, moment = lax.switch(
        step_index[0] % 3, branches, weights, moment, activations, residual, upstream, norm_gain, pattern
    )
    return tuple(a.transpose(2, 0, 1, 3)[None] for a in (weights, moment))


def solution(mesh):
    in_specs = (
        P("rep", None, "fsdp", None),
        P("rep", None, "fsdp", None),
        P("rep", None, "fsdp", None),
        P(),
        P("rep", "fsdp", None, None, None),
        P("rep", "fsdp", None, None, None),
        P(),
        P(),
    )
    out_specs = (P("rep", "fsdp", None, None, None), P("rep", "fsdp", None, None, None))
    return jax.shard_map(body, mesh=mesh, in_specs=in_specs, out_specs=out_specs, check_vma=False)
```
